32 devices in a mesh: txt: 4 (over z), clip: 2 (over x), proj: 4 (over y, core).
Axes of the slice: x: 2, y: 2, z: 4, core: 2. Of those that a mesh axis runs over, the one named last changes fastest.
Arguments:
- text_hidden: float32 [1024, 1024], P(('txt', 'clip')), may hold values from -16 to 16
- proj_weight: float32 [1024, 1024], P(None, 'proj'), may hold values from -2 to 2
- clip_embed: float32 [1024, 1024], P(('txt', 'clip'), 'proj'), may hold values from -16 to 16
- positive: int32 [1024], P(('txt', 'clip')), may hold values from 0 to 1023, each once
- logit_scale: float32 [1], replicated, may hold values from 10 to 300
Outputs:
- grad_hidden: float32 [1024, 1024], P(('txt', 'clip'), 'proj')
- grad_weight: float32 [1024, 1024], P(('txt', 'clip'), 'proj')
- grad_clip: float32 [1024, 1024], P(('txt', 'clip'), 'proj')
The draws below stay inside these ranges and needn't reach their ends.
Inputs may be any that keep to these rules, and one draw needn't show every extreme that they name: `positive`: each clip row is the match of exactly one text row.
All inputs are finite; a program needn't handle non-finite values.
Results may differ from the reference program's by a relative error of at most 0.0003.
Values sent between devices are 32-bit elements; how exact they have to be, the bound alone decides.
No kernel may reach another device: no remote copies, remote signals or barrier semaphores. Data moves between devices by JAX's collectives and lax.ppermute only.
A program may use at most 64 MiB of HBM per device.

```python
import math
import jax
import jax.numpy as jnp
from jax import lax

D = 1024
ROWS = 1024


def row_field(key, salt):
    entry_key, row_key = jax.random.split(jax.random.fold_in(key, salt), 2)
    columns = 1.0 + 2.0 * jnp.arange(D, dtype=jnp.float32) / D
    rescale = jnp.exp(jax.random.uniform(row_key, (ROWS, 1), jnp.float32, math.log(0.1), 0.0))
    entries = jnp.clip(jax.random.normal(entry_key, (ROWS, D), jnp.float32), -5.0, 5.0)
    return entries * rescale * columns[None, :]


def text_base(key):
    base = row_field(key, 101)
    return base


def draw_text_hidden(key, part):
    base = text_base(key)
    return base


def draw_clip_embed(key, part):
    field = row_field(key, 202)
    return field


def draw_proj_weight(key, part):
    noise = jnp.clip(jax.random.normal(jax.random.fold_in(key, 303), (D, D), jnp.float32), -5.0, 5.0) / math.sqrt(D)
    return noise


def draw_logit_scale(key, part):
    scale_key = jax.random.fold_in(key, 404)
    return jax.random.uniform(scale_key, (1,), jnp.float32, 12.0, 30.0)


def setup_inputs(seed: int = 0) -> dict:
    key_of = jax.random.split(jax.random.key(seed), 6)
    return {
        "text_hidden": draw_text_hidden(jax.random.fold_in(key_of[5], 71), 0),
        "proj_weight": draw_proj_weight(jax.random.fold_in(key_of[5], 71), 0),
        "clip_embed": draw_clip_embed(jax.random.fold_in(key_of[5], 71), 0),
        "positive": jax.random.permutation(key_of[3], ROWS).astype(jnp.int32),
        "logit_scale": draw_logit_scale(jax.random.fold_in(key_of[5], 71), 0),
    }


EPSILON = 1e-06
PRECISE = lax.Precision.HIGHEST

def unit_rows(raw):
    inverse = lax.rsqrt(lax.optimization_barrier(jnp.sum(raw * raw, axis=1, keepdims=True)) + EPSILON)
    return (raw * inverse, inverse)

def unit_back(unit, inverse, upstream):
    along = lax.optimization_barrier(jnp.sum(unit * upstream, axis=1, keepdims=True))
    return (upstream - unit * along) * inverse

def reference(text_hidden, proj_weight, clip_embed, positive, logit_scale):
    score_scale = logit_scale[0]
    total_rows = text_hidden.shape[0]
    width = text_hidden.shape[1]
    projected = jnp.dot(text_hidden, proj_weight, precision=PRECISE, preferred_element_type=jnp.float32)
    text_unit, text_inverse = unit_rows(projected)
    clip_unit, clip_inverse = unit_rows(clip_embed)
    block_size = min(total_rows, 1024)
    block_count = total_rows // block_size
    text_blocks = text_unit.reshape(block_count, block_size, width)
    positive_blocks = positive.reshape(block_count, block_size)

    def block_scores(row_block):
        return score_scale * jnp.dot(row_block, clip_unit.T, precision=PRECISE, preferred_element_type=jnp.float32)

    def column_pass(carry, row_block):
        col_max, col_total = carry
        scores = block_scores(row_block)
        new_max = jnp.maximum(col_max, lax.optimization_barrier(jnp.max(scores, axis=0)))
        col_total = col_total * jnp.exp(col_max - new_max) + lax.optimization_barrier(jnp.sum(jnp.exp(scores - new_max[None, :]), axis=0))
        return ((new_max, col_total), None)
    start_max = jnp.full((total_rows,), -jnp.inf, jnp.float32)
    start_total = jnp.zeros((total_rows,), jnp.float32)
    (col_max, col_total), unused = lax.scan(column_pass, (start_max, start_total), text_blocks)

    def gradient_pass(clip_cot, inputs):
        row_block, positive_block = inputs
        scores = block_scores(row_block)
        row_exp = jnp.exp(scores - lax.optimization_barrier(jnp.max(scores, axis=1, keepdims=True)))
        row_prob = row_exp / lax.optimization_barrier(jnp.sum(row_exp, axis=1, keepdims=True))
        col_prob = jnp.exp(scores - col_max[None, :]) / col_total[None, :]
        matches = (lax.broadcasted_iota(jnp.int32, scores.shape, 1) == positive_block[:, None]).astype(jnp.float32)
        grad_scores = 0.5 * (row_prob + col_prob) - matches
        text_cot = score_scale * jnp.dot(grad_scores, clip_unit, precision=PRECISE, preferred_element_type=jnp.float32)
        clip_cot = clip_cot + score_scale * jnp.dot(grad_scores.T, row_block, precision=PRECISE, preferred_element_type=jnp.float32)
        return (clip_cot, text_cot)
    clip_cot, text_cots = lax.scan(gradient_pass, jnp.zeros((total_rows, width), jnp.float32), (text_blocks, positive_blocks))
    text_cot = text_cots.reshape(total_rows, width)
    text_back = unit_back(text_unit, text_inverse, text_cot)
    grad_clip = unit_back(clip_unit, clip_inverse, clip_cot)
    grad_weight = jnp.dot(text_hidden.T, text_back, precision=PRECISE, preferred_element_type=jnp.float32)
    grad_hidden = jnp.dot(text_back, proj_weight.T, precision=PRECISE, preferred_element_type=jnp.float32)
    return (grad_hidden, grad_weight, grad_clip)
```

```python
import jax
import jax.numpy as jnp
from jax import lax
from jax.sharding import PartitionSpec as P

EPSILON = 1e-06
PRECISE = lax.Precision.HIGHEST


def swap(block, *moves):
    axes = tuple(axis for axis, _ in moves)
    sizes = [lax.axis_size(axis) for axis in axes]
    route = []
    total = 1
    for size in sizes:
        total *= size
    for index in range(total):
        rest, coords = index, []
        for size in reversed(sizes):
            coords.insert(0, rest % size)
            rest //= size
        target = 0
        for size, coord, (_, distance) in zip(sizes, coords, moves):
            target = target * size + (coord ^ distance)
        route.append((index, target))
    return lax.ppermute(block, axes if len(axes) > 1 else axes[0], route)


def gather_blocks(block, moves):
    blocks = [block]
    for move in moves:
        if len(blocks) <= 2:
            blocks = blocks + [swap(one, move) for one in blocks]
        else:
            moved = swap(jnp.stack(blocks), move)
            blocks = blocks + [moved[k] for k in range(len(blocks))]
    return blocks


def scatter_blocks(blocks, moves):
    for move in reversed(moves):
        half = len(blocks) // 2
        keep, send = blocks[:half], blocks[half:]
        if half <= 2:
            received = [None] * half
            for k in reversed(range(half)):
                received[k] = swap(send[k], move)
        else:
            moved = swap(jnp.stack(send), move)
            received = [moved[k] for k in range(half)]
        blocks = [one + other for one, other in zip(keep, received)]
    return blocks[0]


def dot(a, b, contract):
    return lax.dot_general(
        a, b, ((contract[0], contract[1]), ((), ())), precision=PRECISE, preferred_element_type=jnp.float32
    )


def merge_stats(mine, other):
    top = jnp.maximum(mine[0], other[0])
    total = mine[1] * jnp.exp(mine[0] - top) + other[1] * jnp.exp(other[0] - top)
    return jnp.stack([top, total])


def flip_bit(stats, bit, blocks):
    step = 1 << bit
    parts = stats.reshape(2, blocks // (2 * step), 2, step, -1)
    return jnp.concatenate([parts[:, :, 1:], parts[:, :, :1]], axis=2).reshape(stats.shape)


def body(text_hidden, proj_weight, clip_embed, positive, logit_scale):
    scale = logit_scale[0]
    txt_n, clip_n = lax.axis_size("txt"), lax.axis_size("clip")
    proj_n = lax.axis_size("proj")
    rows = text_hidden.shape[0]
    width = text_hidden.shape[1]
    feat = proj_weight.shape[1]
    groups = txt_n * clip_n
    txt_bits, clip_bits = txt_n.bit_length() - 1, clip_n.bit_length() - 1
    near = ("txt", 1)
    core = ("proj", 1)
    far = ("proj", 2)
    moves = [("txt", 2 << k) for k in range(txt_bits - 1)] + [("clip", 1 << k) for k in range(clip_bits)]
    weights = [d * clip_n if axis == "txt" else d for axis, d in moves]
    count = len(moves)
    blocks = 1 << count

    own_txt, own_clip, own_proj = lax.axis_index("txt"), lax.axis_index("clip"), lax.axis_index("proj")
    own = own_txt * clip_n + own_clip
    odd = own_proj % 2 == 1

    def offset(q):
        return sum(weights[k] for k in range(count) if q >> k & 1)

    def keep_send(first, second):
        return jnp.where(odd, second, first), jnp.where(odd, first, second)

    clips = gather_blocks(clip_embed, moves)
    projected = dot(text_hidden, proj_weight, ((1,), (0,)))
    projected_near = swap(projected, near)
    positive_near = swap(positive, near)
    raw_keep, raw_send = keep_send(projected, projected_near)
    positive_keep, _ = keep_send(positive, positive_near)

    slot = width // groups
    hidden_blocks = text_hidden.reshape(rows, groups, slot)

    def hidden_columns(base):
        return jnp.concatenate(
            [
                lax.dynamic_index_in_dim(hidden_blocks, base ^ offset(q), axis=1, keepdims=False)
                for q in range(blocks)
            ],
            axis=1,
        )

    hidden_own = hidden_columns(own)
    hidden_near = swap(hidden_columns(own ^ clip_n), near)
    hidden_tile = jnp.concatenate(keep_send(hidden_own, hidden_near), axis=0)

    half = max(blocks // 2, 1)
    raw_scores = []
    for first in range(0, blocks, half):
        clip_part = jnp.concatenate(clips[first : first + half], axis=0)
        sent = swap(dot(raw_send, clip_part, ((1,), (1,))), core)
        part = dot(raw_keep, clip_part, ((1,), (1,))) + sent
        raw_scores.append(part + swap(part, far))
    clip_tile = jnp.concatenate(clips, axis=0)
    raw_text = jnp.concatenate([raw_keep, raw_send], axis=0)
    squares = jnp.concatenate(
        [jnp.sum(raw_keep * raw_keep, axis=1), jnp.sum(raw_send * raw_send, axis=1), jnp.sum(clip_tile * clip_tile, axis=1)]
    )
    flipped = jnp.concatenate([squares[rows : 2 * rows], squares[:rows], squares[2 * rows :]])
    half_sum = squares + swap(flipped, core)
    inverse = lax.rsqrt(half_sum + swap(half_sum, far) + EPSILON)
    text_inverse, clip_inverse = inverse[: 2 * rows], inverse[2 * rows :]
    text_unit = raw_text * text_inverse[:, None]
    clip_unit = clip_tile * clip_inverse[:, None]
    scores = (
        jnp.concatenate(raw_scores, axis=1) * (scale * text_inverse[:rows])[:, None] * clip_inverse[None, :]
    )

    row_max = jnp.max(scores, axis=1)
    col_max = jnp.max(scores, axis=0)
    row_stats = jnp.stack([row_max, jnp.sum(jnp.exp(scores - row_max[:, None]), axis=1)])
    col_stats = jnp.stack([col_max, jnp.sum(jnp.exp(scores - col_max[None, :]), axis=0)])
    row_stats = merge_stats(row_stats, swap(row_stats, near, core))
    col_stats = merge_stats(col_stats, swap(col_stats, core))
    for k in reversed(range(count)):
        col_stats = merge_stats(col_stats, flip_bit(swap(col_stats, moves[k]), k, blocks))

    relative = positive_keep // rows ^ own
    position = sum(((relative // weights[k]) % 2) << k for k in range(count))
    inside = (relative // clip_n) % 2 == 0
    column = jnp.where(inside, position * rows + positive_keep % rows, -1)
    matches = (lax.broadcasted_iota(jnp.int32, scores.shape, 1) == column[:, None]).astype(jnp.float32)
    grad = (
        0.5
        * (
            jnp.exp(scores - row_stats[0][:, None]) / row_stats[1][:, None]
            + jnp.exp(scores - col_stats[0][None, :]) / col_stats[1][None, :]
        )
        - matches
    )
    along = jnp.concatenate([jnp.sum(grad * scores, axis=1), jnp.sum(grad * scores, axis=0)])
    grad_tile = jnp.concatenate([grad, swap(grad, core)], axis=0)
    along_other = swap(along, core)
    text_along = jnp.concatenate([along[:rows], along_other[:rows]])
    clip_along = along[rows:] + along_other[rows:]

    text_part = scale * dot(grad_tile, clip_unit, ((1,), (0,)))
    text_other = swap(text_part, near)
    text_cot = text_part + jnp.concatenate([text_other[rows:], text_other[:rows]], axis=0)
    along_near = swap(text_along, near)
    text_along = text_along + jnp.concatenate([along_near[rows:], along_near[:rows]])
    clip_part = scale * dot(grad_tile, text_unit, ((0,), (0,)))
    clip_cot = scatter_blocks([clip_part[q * rows : (q + 1) * rows] for q in range(blocks)], moves)
    clip_along = scatter_blocks([clip_along[q * rows : (q + 1) * rows] for q in range(blocks)], moves)

    text_back = (text_cot - text_unit * text_along[:, None]) * text_inverse[:, None]
    grad_clip = (clip_cot - clip_unit[:rows] * clip_along[:, None]) * clip_inverse[:rows, None]

    weight_part = dot(hidden_tile, text_back, ((0,), (0,)))
    grad_weight = scatter_blocks([weight_part[q * slot : (q + 1) * slot] for q in range(blocks)], moves)

    own_back = jnp.where(odd, text_back[rows:], text_back[:rows])
    weight_rows = proj_weight.reshape(proj_n, width // proj_n, feat)
    hidden_parts = [
        dot(own_back, lax.dynamic_index_in_dim(weight_rows, own_proj ^ (2 * (q & 1) + (q >> 1)), axis=0, keepdims=False), ((1,), (1,)))
        for q in range(proj_n)
    ]
    grad_hidden = scatter_blocks(hidden_parts, [far, core])
    return (grad_hidden, grad_weight, grad_clip)


def solution(mesh):
    in_specs = (
        P(("txt", "clip"), None),
        P(None, "proj"),
        P(("txt", "clip"), "proj"),
        P(("txt", "clip")),
        P(),
    )
    out_specs = (P(("txt", "clip"), "proj"), P(("txt", "clip"), "proj"), P(("txt", "clip"), "proj"))
    return jax.shard_map(body, mesh=mesh, in_specs=in_specs, out_specs=out_specs, check_vma=False)
```

```python
import jax
import jax.numpy as jnp
from jax import lax
from jax.sharding import PartitionSpec as P

EPSILON = 1e-06
PRECISE = lax.Precision.HIGH


def swap(block, *moves):
    axes = tuple(axis for axis, _ in moves)
    sizes = [lax.axis_size(axis) for axis in axes]
    route = []
    total = 1
    for size in sizes:
        total *= size
    for index in range(total):
        rest, coords = index, []
        for size in reversed(sizes):
            coords.insert(0, rest % size)
            rest //= size
        target = 0
        for size, coord, (_, distance) in zip(sizes, coords, moves):
            target = target * size + (coord ^ distance)
        route.append((index, target))
    return lax.ppermute(block, axes if len(axes) > 1 else axes[0], route)


def gather_blocks(block, moves):
    blocks = [block]
    for move in moves:
        if len(blocks) <= 2:
            blocks = blocks + [swap(one, move) for one in blocks]
        else:
            moved = swap(jnp.stack(blocks), move)
            blocks = blocks + [moved[k] for k in range(len(blocks))]
    return blocks


def scatter_blocks(blocks, moves):
    for level in reversed(range(len(moves))):
        half = len(blocks) // 2
        keep, send = blocks[:half], blocks[half:]
        if half <= 2:
            received = [None] * half
            for k in reversed(range(half)):
                received[k] = swap(send[k], moves[level])
        else:
            moved = swap(jnp.stack(send), moves[level])
            received = [moved[k] for k in range(half)]
        blocks = [one + other for one, other in zip(keep, received)]
    return blocks[0]


def dot(a, b, contract):
    return lax.dot_general(
        a, b, ((contract[0], contract[1]), ((), ())), precision=PRECISE, preferred_element_type=jnp.float32
    )


def merge_stats(mine, other):
    top = jnp.maximum(mine[0], other[0])
    total = mine[1] * jnp.exp(mine[0] - top) + other[1] * jnp.exp(other[0] - top)
    return jnp.stack([top, total])


def flip_blocks(stats, q, blocks):
    size = stats.shape[1] // blocks
    order = [k ^ q for k in range(blocks)]
    return jnp.concatenate([stats[:, k * size : (k + 1) * size] for k in order], axis=1)


def body(text_hidden, proj_weight, clip_embed, positive, logit_scale):
    scale = logit_scale[0]
    txt_n, clip_n = lax.axis_size("txt"), lax.axis_size("clip")
    proj_n = lax.axis_size("proj")
    rows = text_hidden.shape[0]
    width = text_hidden.shape[1]
    feat = proj_weight.shape[1]
    groups = txt_n * clip_n
    txt_bits, clip_bits = txt_n.bit_length() - 1, clip_n.bit_length() - 1
    near = ("txt", 1)
    core = ("proj", 1)
    far = ("proj", 2)
    moves = [("txt", 2 << k) for k in range(txt_bits - 1)] + [("clip", 1 << k) for k in range(clip_bits)]
    weights = [d * clip_n if axis == "txt" else d for axis, d in moves]
    count = len(moves)
    blocks = 1 << count
    part = rows // 2

    own_txt, own_clip, own_proj = lax.axis_index("txt"), lax.axis_index("clip"), lax.axis_index("proj")
    own = own_txt * clip_n + own_clip
    own_core = own_proj % 2

    def offset(q):
        return sum(weights[k] for k in range(count) if q >> k & 1)

    clips = gather_blocks(clip_embed, moves)
    clip_keep, clip_send = [], []
    for one in clips:
        clip_keep.append(lax.dynamic_slice_in_dim(one, own_core * part, part))
        clip_send.append(lax.dynamic_slice_in_dim(one, (1 - own_core) * part, part))
    projected = dot(text_hidden, proj_weight, ((1,), (0,)))
    upper = own_txt % 2

    def pair_rows(mine, other):
        whole = jnp.zeros((2 * rows,) + mine.shape[1:], mine.dtype)
        whole = lax.dynamic_update_slice_in_dim(whole, mine, upper * rows, 0)
        return lax.dynamic_update_slice_in_dim(whole, other, (1 - upper) * rows, 0)

    projected_near = swap(projected, near)
    text_raw = pair_rows(projected, projected_near)

    slot = width // groups
    hidden_blocks = text_hidden.reshape(rows, groups, slot)

    def hidden_columns(base):
        return jnp.concatenate(
            [
                lax.dynamic_index_in_dim(hidden_blocks, base ^ offset(q), axis=1, keepdims=False)
                for q in range(blocks)
            ],
            axis=1,
        )

    half_width = blocks * slot
    spare = -(-rows // half_width)
    match_rows = jnp.pad(positive.astype(jnp.float32), (0, spare * half_width - rows)).reshape(spare, half_width)
    hidden_near = swap(jnp.concatenate([hidden_columns(own ^ clip_n), match_rows], axis=0), near)
    hidden_tile = pair_rows(hidden_columns(own), hidden_near[:rows])
    match_near = hidden_near[rows:].reshape(-1)[:rows].astype(jnp.int32)
    matching = jnp.where(upper == 0, jnp.concatenate([positive, match_near]), jnp.concatenate([match_near, positive]))

    cut = blocks - max(blocks // 4, 1)
    half = blocks * part
    keep_tile = jnp.concatenate(clip_keep, axis=0)
    send_tile = jnp.concatenate(clip_send, axis=0)
    squares = [jnp.sum(text_raw * text_raw, axis=1)]
    squares += [jnp.sum(one * one, axis=1) for one in (keep_tile, send_tile)]
    half_rows = -(-half // (2 * rows))

    def as_rows(values):
        size = -(-values.shape[0] // (2 * rows)) * 2 * rows
        return jnp.pad(values, (0, size - values.shape[0])).reshape(-1, 2 * rows)

    squares = [as_rows(one) for one in squares]
    spare_rows = -(-(1 + 2 * half_rows) // 8) * 8

    def with_squares(part_scores, values):
        whole = jnp.zeros((part_scores.shape[0] + spare_rows, 2 * rows), jnp.float32)
        whole = lax.dynamic_update_slice(whole, part_scores, (0, 0))
        return lax.dynamic_update_slice(whole, values, (part_scores.shape[0], 0))

    raw_scores = []
    for k, span in enumerate((slice(0, cut), slice(cut, blocks))):
        keep = jnp.concatenate(clip_keep[span], axis=0)
        send = jnp.concatenate(clip_send[span], axis=0)
        lanes = keep.shape[0]
        part_scores = dot(send, text_raw, ((1,), (1,)))
        if k == 1:
            part_scores = with_squares(part_scores, jnp.concatenate([squares[0], squares[2], squares[1]], axis=0))
        sent = swap(part_scores, core)
        mine = dot(keep, text_raw, ((1,), (1,))) + sent[:lanes]
        if k == 1:
            square_sum = jnp.concatenate(squares, axis=0) + sent[lanes : lanes + 1 + 2 * half_rows]
            mine = with_squares(mine, square_sum)
        mine = mine + swap(mine, far)
        raw_scores.append(mine[:lanes])
    inverse = lax.rsqrt(mine[lanes : lanes + 1 + 2 * half_rows] + EPSILON)
    text_inverse = inverse[0][:, None]
    keep_inverse = inverse[1 : 1 + half_rows].reshape(-1)[:half, None]
    send_inverse = inverse[1 + half_rows :].reshape(-1)[:half, None]
    text_unit = text_raw * text_inverse
    keep_unit = keep_tile * keep_inverse
    send_unit = send_tile * send_inverse
    scores = jnp.concatenate(raw_scores, axis=0) * keep_inverse * (scale * inverse[:1])

    row_max = jnp.max(scores, axis=0)
    col_max = jnp.max(scores, axis=1)
    row_stats = jnp.stack([row_max, jnp.sum(jnp.exp(scores - row_max[None, :]), axis=0)])
    col_stats = jnp.stack([col_max, jnp.sum(jnp.exp(scores - col_max[:, None]), axis=1)])
    row_stats = merge_stats(row_stats, swap(row_stats, core))
    row_stats = merge_stats(row_stats, swap(row_stats, near))
    for k in reversed(range(count)):
        col_stats = merge_stats(col_stats, flip_blocks(swap(col_stats, moves[k]), 1 << k, blocks))

    row_bits, part_bits = rows.bit_length() - 1, part.bit_length() - 1
    relative = lax.shift_right_logical(matching, row_bits) ^ own
    entry = matching & (rows - 1)
    position = entry & (part - 1)
    for k in range(count):
        bit = lax.shift_right_logical(relative, weights[k].bit_length() - 1) & 1
        position = position | (bit << (k + part_bits))
    inside = ((relative >> clip_bits) & 1 == 0) & (entry >> part_bits == own_core)
    column = jnp.where(inside, position, -1)
    matches = (lax.broadcasted_iota(jnp.int32, scores.shape, 0) == column[None, :]).astype(jnp.float32)
    grad = (
        0.5
        * (
            jnp.exp(scores - row_stats[0][None, :]) / row_stats[1][None, :]
            + jnp.exp(scores - col_stats[0][:, None]) / col_stats[1][:, None]
        )
        - matches
    )
    weighted = grad * scores
    along = jnp.concatenate([jnp.sum(weighted, axis=0), jnp.sum(weighted, axis=1)])
    grad_other = swap(grad, core)
    along_other = swap(along, core)
    text_along = (along[: 2 * rows] + along_other[: 2 * rows])[:, None]
    keep_along, send_along = along[2 * rows :, None], along_other[2 * rows :, None]

    text_mine = lax.optimization_barrier(dot(grad, keep_unit, ((0,), (0,))))
    text_parts = []
    for k in range(2):
        cols = slice(k * (feat // 2), (k + 1) * (feat // 2))
        cot = text_mine[:, cols] + dot(grad_other, send_unit[:, cols], ((0,), (0,)))
        text_parts.append((scale * cot - text_unit[:, cols] * text_along) * text_inverse)
    text_back = [one + swap(one, near) for one in text_parts]
    keep_back = (scale * dot(grad, text_unit, ((1,), (0,))) - keep_unit * keep_along) * keep_inverse
    send_back = (scale * dot(grad_other, text_unit, ((1,), (0,))) - send_unit * send_along) * send_inverse
    clip_back = scatter_blocks(
        [
            jnp.concatenate([keep_back[q * part : (q + 1) * part], send_back[q * part : (q + 1) * part]], axis=0)
            for q in range(blocks)
        ],
        moves,
    )
    grad_clip = jnp.where(own_core == 0, clip_back, jnp.concatenate([clip_back[part:], clip_back[:part]], axis=0))

    top = blocks // 2
    outer = [q for q in range(blocks) if q & 1]
    inner = [q for q in range(blocks) if not q & 1]

    def hidden_of(which):
        return jnp.concatenate([hidden_tile[:, q * slot : (q + 1) * slot] for q in which], axis=1)

    halves = []
    for k in range(2):
        crossing = dot(hidden_of(outer), text_back[k], ((0,), (0,)))
        crossing = scatter_blocks([crossing[j * slot : (j + 1) * slot] for j in range(top)], moves[1:])
        halves.append(swap(crossing, moves[0]))
    text_back = jnp.concatenate(text_back, axis=1)
    rest = dot(hidden_of(inner), text_back, ((0,), (0,)))
    rest = scatter_blocks([rest[j * slot : (j + 1) * slot] for j in range(top)], moves[1:])
    grad_weight = rest + jnp.concatenate(halves, axis=1)

    own_back = lax.dynamic_slice_in_dim(text_back, upper * rows, rows)
    hidden_part = dot(own_back, proj_weight, ((1,), (1,)))
    piece = width // proj_n
    hidden_parts = [
        lax.dynamic_slice_in_dim(hidden_part, (own_proj ^ (2 * (q & 1) + (q >> 1))) * piece, piece, axis=1)
        for q in range(proj_n)
    ]
    grad_hidden = scatter_blocks(hidden_parts, [far, core])
    return (grad_hidden, grad_weight, grad_clip)


def solution(mesh):
    in_specs = (
        P(("txt", "clip"), None),
        P(None, "proj"),
        P(("txt", "clip"), "proj"),
        P(("txt", "clip")),
        P(),
    )
    out_specs = (P(("txt", "clip"), "proj"), P(("txt", "clip"), "proj"), P(("txt", "clip"), "proj"))
    return jax.shard_map(body, mesh=mesh, in_specs=in_specs, out_specs=out_specs, check_vma=False)
```

```python
import jax
import jax.numpy as jnp
from jax import lax
from jax.sharding import PartitionSpec as P

EPSILON = 1e-06
PRECISE = lax.Precision.HIGH


def swap(block, *moves):
    axes = tuple(axis for axis, _ in moves)
    sizes = [lax.axis_size(axis) for axis in axes]
    route = []
    total = 1
    for size in sizes:
        total *= size
    for index in range(total):
        rest, coords = index, []
        for size in reversed(sizes):
            coords.insert(0, rest % size)
            rest //= size
        target = 0
        for size, coord, (_, distance) in zip(sizes, coords, moves):
            target = target * size + (coord ^ distance)
        route.append((index, target))
    return lax.ppermute(block, axes if len(axes) > 1 else axes[0], route)


def gather_blocks(block, moves):
    blocks = [block]
    for move in moves:
        if len(blocks) <= 2:
            blocks = blocks + [swap(one, move) for one in blocks]
        else:
            moved = swap(jnp.stack(blocks), move)
            blocks = blocks + [moved[k] for k in range(len(blocks))]
    return blocks


def scatter_blocks(blocks, moves):
    for level in reversed(range(len(moves))):
        half = len(blocks) // 2
        keep, send = blocks[:half], blocks[half:]
        if half <= 2:
            received = [None] * half
            for k in reversed(range(half)):
                received[k] = swap(send[k], moves[level])
        else:
            moved = swap(jnp.stack(send), moves[level])
            received = [moved[k] for k in range(half)]
        blocks = [one + other for one, other in zip(keep, received)]
    return blocks[0]


def dot(a, b, contract):
    return lax.dot_general(
        a, b, ((contract[0], contract[1]), ((), ())), precision=PRECISE, preferred_element_type=jnp.float32
    )


def merge_stats(mine, other):
    top = jnp.maximum(mine[0], other[0])
    total = mine[1] * jnp.exp(mine[0] - top) + other[1] * jnp.exp(other[0] - top)
    return jnp.stack([top, total])


def flip_blocks(stats, q, blocks):
    size = stats.shape[1] // blocks
    order = [k ^ q for k in range(blocks)]
    return jnp.concatenate([stats[:, k * size : (k + 1) * size] for k in order], axis=1)


def body(text_hidden, proj_weight, clip_embed, positive, logit_scale):
    scale = logit_scale[0]
    txt_n, clip_n = lax.axis_size("txt"), lax.axis_size("clip")
    proj_n = lax.axis_size("proj")
    rows = text_hidden.shape[0]
    width = text_hidden.shape[1]
    feat = proj_weight.shape[1]
    groups = txt_n * clip_n
    txt_bits, clip_bits = txt_n.bit_length() - 1, clip_n.bit_length() - 1
    near = ("txt", 1)
    core = ("proj", 1)
    far = ("proj", 2)
    moves = [("txt", 2 << k) for k in range(txt_bits - 1)] + [("clip", 1 << k) for k in range(clip_bits)]
    weights = [d * clip_n if axis == "txt" else d for axis, d in moves]
    count = len(moves)
    blocks = 1 << count
    part = rows // 2

    own_txt, own_clip, own_proj = lax.axis_index("txt"), lax.axis_index("clip"), lax.axis_index("proj")
    own = own_txt * clip_n + own_clip
    own_core = own_proj % 2

    def offset(q):
        return sum(weights[k] for k in range(count) if q >> k & 1)

    clips = gather_blocks(clip_embed, moves)
    clip_keep, clip_send = [], []
    for one in clips:
        clip_keep.append(lax.dynamic_slice_in_dim(one, own_core * part, part))
        clip_send.append(lax.dynamic_slice_in_dim(one, (1 - own_core) * part, part))
    projected = dot(text_hidden, proj_weight, ((1,), (0,)))
    upper = own_txt % 2

    def pair_rows(mine, other):
        whole = jnp.zeros((2 * rows,) + mine.shape[1:], mine.dtype)
        whole = lax.dynamic_update_slice_in_dim(whole, mine, upper * rows, 0)
        return lax.dynamic_update_slice_in_dim(whole, other, (1 - upper) * rows, 0)

    projected_near = swap(projected, near)
    text_raw = pair_rows(projected, projected_near)

    slot = width // groups
    hidden_blocks = text_hidden.reshape(rows, groups, slot)

    def hidden_columns(base):
        return jnp.concatenate(
            [
                lax.dynamic_index_in_dim(hidden_blocks, base ^ offset(q), axis=1, keepdims=False)
                for q in range(blocks)
            ],
            axis=1,
        )

    half_width = blocks * slot
    spare = -(-rows // half_width)
    match_rows = jnp.pad(positive.astype(jnp.float32), (0, spare * half_width - rows)).reshape(spare, half_width)
    hidden_near = swap(jnp.concatenate([hidden_columns(own ^ clip_n), match_rows], axis=0), near)
    hidden_tile = pair_rows(hidden_columns(own), hidden_near[:rows])
    match_near = hidden_near[rows:].reshape(-1)[:rows].astype(jnp.int32)
    matching = jnp.where(upper == 0, jnp.concatenate([positive, match_near]), jnp.concatenate([match_near, positive]))

    cut = blocks - max(blocks // 4, 1)
    half = blocks * part
    keep_tile = jnp.concatenate(clip_keep, axis=0)
    send_tile = jnp.concatenate(clip_send, axis=0)
    squares = [jnp.sum(text_raw * text_raw, axis=1)]
    squares += [jnp.sum(one * one, axis=1) for one in (keep_tile, send_tile)]
    half_rows = -(-half // (2 * rows))

    def as_rows(values):
        size = -(-values.shape[0] // (2 * rows)) * 2 * rows
        return jnp.pad(values, (0, size - values.shape[0])).reshape(-1, 2 * rows)

    squares = [as_rows(one) for one in squares]
    spare_rows = -(-(1 + 2 * half_rows) // 8) * 8

    def with_rows(block, values):
        whole = jnp.zeros((block.shape[0] + spare_rows, 2 * rows), jnp.float32)
        whole = lax.dynamic_update_slice(whole, block, (0, 0))
        return lax.dynamic_update_slice(whole, values, (block.shape[0], 0))

    raw_scores = []
    for k, span in enumerate((slice(0, cut), slice(cut, blocks))):
        keep = jnp.concatenate(clip_keep[span], axis=0)
        send = jnp.concatenate(clip_send[span], axis=0)
        lanes = keep.shape[0]
        part_scores = dot(send, text_raw, ((1,), (1,)))
        if k == 1:
            part_scores = with_rows(part_scores, jnp.concatenate([squares[0], squares[2], squares[1]], axis=0))
        sent = swap(part_scores, core)
        mine = dot(keep, text_raw, ((1,), (1,))) + sent[:lanes]
        if k == 1:
            square_sum = jnp.concatenate(squares, axis=0) + sent[lanes : lanes + 1 + 2 * half_rows]
            mine = with_rows(mine, square_sum)
        mine = mine + swap(mine, far)
        raw_scores.append(mine[:lanes])
    inverse = lax.rsqrt(mine[lanes : lanes + 1 + 2 * half_rows] + EPSILON)
    text_inverse = inverse[0][:, None]
    keep_inverse = inverse[1 : 1 + half_rows].reshape(-1)[:half, None]
    send_inverse = inverse[1 + half_rows :].reshape(-1)[:half, None]
    text_unit = text_raw * text_inverse
    keep_unit = keep_tile * keep_inverse
    send_unit = send_tile * send_inverse
    scores = jnp.concatenate(raw_scores, axis=0) * keep_inverse * (scale * inverse[:1])

    row_max = jnp.max(scores, axis=0)
    col_max = jnp.max(scores, axis=1)
    row_stats = jnp.stack([row_max, jnp.sum(jnp.exp(scores - row_max[None, :]), axis=0)])
    col_stats = jnp.stack([col_max, jnp.sum(jnp.exp(scores - col_max[:, None]), axis=1)])
    row_stats = merge_stats(row_stats, swap(row_stats, core))
    row_stats = merge_stats(row_stats, swap(row_stats, near))
    for k in reversed(range(count)):
        col_stats = merge_stats(col_stats, flip_blocks(swap(col_stats, moves[k]), 1 << k, blocks))

    row_bits, part_bits = rows.bit_length() - 1, part.bit_length() - 1
    relative = lax.shift_right_logical(matching, row_bits) ^ own
    entry = matching & (rows - 1)
    position = entry & (part - 1)
    for k in range(count):
        bit = lax.shift_right_logical(relative, weights[k].bit_length() - 1) & 1
        position = position | (bit << (k + part_bits))
    inside = ((relative >> clip_bits) & 1 == 0) & (entry >> part_bits == own_core)
    column = jnp.where(inside, position, -1)
    matches = (lax.broadcasted_iota(jnp.int32, scores.shape, 0) == column[None, :]).astype(jnp.float32)
    grad = (
        0.5
        * (
            jnp.exp(scores - row_stats[0][None, :]) / row_stats[1][None, :]
            + jnp.exp(scores - col_stats[0][:, None]) / col_stats[1][:, None]
        )
        - matches
    )
    weighted = grad * scores
    along = jnp.concatenate([as_rows(jnp.sum(weighted, axis=0)), as_rows(jnp.sum(weighted, axis=1))], axis=0)
    moved = swap(with_rows(grad, along), core)
    grad_other, along_other = moved[:half], moved[half : half + 1 + half_rows]
    text_along = (along[0] + along_other[0])[:, None]
    keep_along = along[1:].reshape(-1)[:half, None]
    send_along = along_other[1:].reshape(-1)[:half, None]

    text_mine = lax.optimization_barrier(dot(grad, keep_unit, ((0,), (0,))))
    text_parts = []
    for _ in range(1):
        cols = slice(0, feat)
        cot = text_mine[:, cols] + dot(grad_other, send_unit[:, cols], ((0,), (0,)))
        text_parts.append((scale * cot - text_unit[:, cols] * text_along) * text_inverse)
    text_back = [one + swap(one, near) for one in text_parts]
    keep_back = (scale * dot(grad, text_unit, ((1,), (0,))) - keep_unit * keep_along) * keep_inverse
    send_back = (scale * dot(grad_other, text_unit, ((1,), (0,))) - send_unit * send_along) * send_inverse
    clip_back = scatter_blocks(
        [
            jnp.concatenate([keep_back[q * part : (q + 1) * part], send_back[q * part : (q + 1) * part]], axis=0)
            for q in range(blocks)
        ],
        moves,
    )
    grad_clip = jnp.where(own_core == 0, clip_back, jnp.concatenate([clip_back[part:], clip_back[:part]], axis=0))

    top = blocks // 2
    outer = [q for q in range(blocks) if q & 1]
    inner = [q for q in range(blocks) if not q & 1]

    def hidden_of(which):
        return jnp.concatenate([hidden_tile[:, q * slot : (q + 1) * slot] for q in which], axis=1)

    halves = []
    for k in range(1):
        crossing = dot(hidden_of(outer), text_back[k], ((0,), (0,)))
        crossing = scatter_blocks([crossing[j * slot : (j + 1) * slot] for j in range(top)], moves[1:])
        halves.append(swap(crossing, moves[0]))
    text_back = jnp.concatenate(text_back, axis=1)
    rest = dot(hidden_of(inner), text_back, ((0,), (0,)))
    rest = scatter_blocks([rest[j * slot : (j + 1) * slot] for j in range(top)], moves[1:])
    grad_weight = rest + jnp.concatenate(halves, axis=1)

    own_back = lax.dynamic_slice_in_dim(text_back, upper * rows, rows)
    hidden_part = dot(own_back, proj_weight, ((1,), (1,)))
    piece = width // proj_n
    hidden_parts = [
        lax.dynamic_slice_in_dim(hidden_part, (own_proj ^ (2 * (q & 1) + (q >> 1))) * piece, piece, axis=1)
        for q in range(proj_n)
    ]
    grad_hidden = scatter_blocks(hidden_parts, [far, core])
    return (grad_hidden, grad_weight, grad_clip)


def solution(mesh):
    in_specs = (
        P(("txt", "clip"), None),
        P(None, "proj"),
        P(("txt", "clip"), "proj"),
        P(("txt", "clip")),
        P(),
    )
    out_specs = (P(("txt", "clip"), "proj"), P(("txt", "clip"), "proj"), P(("txt", "clip"), "proj"))
    return jax.shard_map(body, mesh=mesh, in_specs=in_specs, out_specs=out_specs, check_vma=False)
```

```python
import jax
import jax.numpy as jnp
from jax import lax
from jax.sharding import PartitionSpec as P

EPSILON = 1e-06
PRECISE = lax.Precision.HIGH


def swap(block, *moves):
    axes = tuple(axis for axis, _ in moves)
    sizes = [lax.axis_size(axis) for axis in axes]
    route = []
    total = 1
    for size in sizes:
        total *= size
    for index in range(total):
        rest, coords = index, []
        for size in reversed(sizes):
            coords.insert(0, rest % size)
            rest //= size
        target = 0
        for size, coord, (_, distance) in zip(sizes, coords, moves):
            target = target * size + (coord ^ distance)
        route.append((index, target))
    return lax.ppermute(block, axes if len(axes) > 1 else axes[0], route)


def gather_blocks(block, moves):
    blocks = [block]
    for move in moves:
        if len(blocks) <= 2:
            blocks = blocks + [swap(one, move) for one in blocks]
        else:
            moved = swap(jnp.stack(blocks), move)
            blocks = blocks + [moved[k] for k in range(len(blocks))]
    return blocks


def scatter_blocks(blocks, moves):
    for level in reversed(range(len(moves))):
        half = len(blocks) // 2
        keep, send = blocks[:half], blocks[half:]
        if half <= 2:
            received = [None] * half
            for k in reversed(range(half)):
                received[k] = swap(send[k], moves[level])
        else:
            moved = swap(jnp.stack(send), moves[level])
            received = [moved[k] for k in range(half)]
        blocks = [one + other for one, other in zip(keep, received)]
    return blocks[0]


def dot(a, b, contract):
    return lax.dot_general(
        a, b, ((contract[0], contract[1]), ((), ())), precision=PRECISE, preferred_element_type=jnp.float32
    )


def merge_stats(mine, other):
    top = jnp.maximum(mine[0], other[0])
    total = mine[1] * jnp.exp(mine[0] - top) + other[1] * jnp.exp(other[0] - top)
    return jnp.stack([top, total])


def flip_blocks(stats, q, blocks):
    size = stats.shape[1] // blocks
    order = [k ^ q for k in range(blocks)]
    return jnp.concatenate([stats[:, k * size : (k + 1) * size] for k in order], axis=1)


def body(text_hidden, proj_weight, clip_embed, positive, logit_scale):
    scale = logit_scale[0]
    txt_n, clip_n = lax.axis_size("txt"), lax.axis_size("clip")
    proj_n = lax.axis_size("proj")
    rows = text_hidden.shape[0]
    width = text_hidden.shape[1]
    feat = proj_weight.shape[1]
    groups = txt_n * clip_n
    txt_bits, clip_bits = txt_n.bit_length() - 1, clip_n.bit_length() - 1
    near = ("txt", 1)
    core = ("proj", 1)
    far = ("proj", 2)
    moves = [("txt", 2 << k) for k in range(txt_bits - 1)] + [("clip", 1 << k) for k in range(clip_bits)]
    weights = [d * clip_n if axis == "txt" else d for axis, d in moves]
    count = len(moves)
    blocks = 1 << count
    part = rows // 2

    own_txt, own_clip, own_proj = lax.axis_index("txt"), lax.axis_index("clip"), lax.axis_index("proj")
    own = own_txt * clip_n + own_clip
    own_core = own_proj % 2

    def offset(q):
        return sum(weights[k] for k in range(count) if q >> k & 1)

    clips = gather_blocks(clip_embed, moves)
    clip_keep, clip_send = [], []
    for one in clips:
        clip_keep.append(lax.dynamic_slice_in_dim(one, own_core * part, part))
        clip_send.append(lax.dynamic_slice_in_dim(one, (1 - own_core) * part, part))
    projected = dot(text_hidden, proj_weight, ((1,), (0,)))
    upper = own_txt % 2

    def pair_rows(mine, other):
        whole = jnp.zeros((2 * rows,) + mine.shape[1:], mine.dtype)
        whole = lax.dynamic_update_slice_in_dim(whole, mine, upper * rows, 0)
        return lax.dynamic_update_slice_in_dim(whole, other, (1 - upper) * rows, 0)

    projected_near = swap(projected, near)
    text_raw = pair_rows(projected, projected_near)

    slot = width // groups
    hidden_blocks = text_hidden.reshape(rows, groups, slot)

    def hidden_columns(base):
        return jnp.concatenate(
            [
                lax.dynamic_index_in_dim(hidden_blocks, base ^ offset(q), axis=1, keepdims=False)
                for q in range(blocks)
            ],
            axis=1,
        )

    half_width = blocks * slot
    spare = -(-rows // half_width)
    match_rows = jnp.pad(positive.astype(jnp.float32), (0, spare * half_width - rows)).reshape(spare, half_width)
    hidden_near = swap(jnp.concatenate([hidden_columns(own ^ clip_n), match_rows], axis=0), near)
    hidden_tile = pair_rows(hidden_columns(own), hidden_near[:rows])
    match_near = hidden_near[rows:].reshape(-1)[:rows].astype(jnp.int32)
    matching = jnp.where(upper == 0, jnp.concatenate([positive, match_near]), jnp.concatenate([match_near, positive]))

    cut = blocks - max(blocks // 4, 1)
    half = blocks * part
    keep_tile = jnp.concatenate(clip_keep, axis=0)
    send_tile = jnp.concatenate(clip_send, axis=0)
    squares = [jnp.sum(text_raw * text_raw, axis=1)]
    squares += [jnp.sum(one * one, axis=1) for one in (keep_tile, send_tile)]
    half_rows = -(-half // (2 * rows))

    def as_rows(values):
        size = -(-values.shape[0] // (2 * rows)) * 2 * rows
        return jnp.pad(values, (0, size - values.shape[0])).reshape(-1, 2 * rows)

    squares = [as_rows(one) for one in squares]
    spare_rows = -(-(1 + 2 * half_rows) // 8) * 8

    def with_rows(block, values):
        whole = jnp.zeros((block.shape[0] + spare_rows, 2 * rows), jnp.float32)
        whole = lax.dynamic_update_slice(whole, block, (0, 0))
        return lax.dynamic_update_slice(whole, values, (block.shape[0], 0))

    raw_scores = []
    for k, span in enumerate((slice(0, cut), slice(cut, blocks))):
        keep = jnp.concatenate(clip_keep[span], axis=0)
        send = jnp.concatenate(clip_send[span], axis=0)
        lanes = keep.shape[0]
        part_scores = dot(send, text_raw, ((1,), (1,)))
        if k == 1:
            part_scores = with_rows(part_scores, jnp.concatenate([squares[0], squares[2], squares[1]], axis=0))
        sent = swap(part_scores, core)
        mine = dot(keep, text_raw, ((1,), (1,))) + sent[:lanes]
        if k == 1:
            square_sum = jnp.concatenate(squares, axis=0) + sent[lanes : lanes + 1 + 2 * half_rows]
            mine = with_rows(mine, square_sum)
        mine = mine + swap(mine, far)
        raw_scores.append(mine[:lanes])
    inverse = lax.rsqrt(mine[lanes : lanes + 1 + 2 * half_rows] + EPSILON)
    text_inverse = inverse[0][:, None]
    keep_inverse = inverse[1 : 1 + half_rows].reshape(-1)[:half, None]
    send_inverse = inverse[1 + half_rows :].reshape(-1)[:half, None]
    text_unit = text_raw * text_inverse
    keep_unit = keep_tile * keep_inverse
    send_unit = send_tile * send_inverse
    scores = jnp.concatenate(raw_scores, axis=0) * keep_inverse * (scale * inverse[:1])

    row_max = jnp.max(scores, axis=0)
    col_max = jnp.max(scores, axis=1)
    row_stats = jnp.stack([row_max, jnp.sum(jnp.exp(scores - row_max[None, :]), axis=0)])
    col_stats = jnp.stack([col_max, jnp.sum(jnp.exp(scores - col_max[:, None]), axis=1)])
    row_stats = merge_stats(row_stats, swap(row_stats, core))
    row_stats = merge_stats(row_stats, swap(row_stats, near))
    for k in reversed(range(count)):
        col_stats = merge_stats(col_stats, flip_blocks(swap(col_stats, moves[k]), 1 << k, blocks))

    row_bits, part_bits = rows.bit_length() - 1, part.bit_length() - 1
    relative = lax.shift_right_logical(matching, row_bits) ^ own
    entry = matching & (rows - 1)
    position = entry & (part - 1)
    for k in range(count):
        bit = lax.shift_right_logical(relative, weights[k].bit_length() - 1) & 1
        position = position | (bit << (k + part_bits))
    inside = ((relative >> clip_bits) & 1 == 0) & (entry >> part_bits == own_core)
    column = jnp.where(inside, position, -1)
    matches = (lax.broadcasted_iota(jnp.int32, scores.shape, 0) == column[None, :]).astype(jnp.float32)
    grad = (
        0.5
        * (
            jnp.exp(scores - row_stats[0][None, :]) / row_stats[1][None, :]
            + jnp.exp(scores - col_stats[0][:, None]) / col_stats[1][:, None]
        )
        - matches
    )
    weighted = grad * scores
    along = jnp.concatenate([as_rows(jnp.sum(weighted, axis=0)), as_rows(jnp.sum(weighted, axis=1))], axis=0)
    moved = swap(with_rows(grad, along), core)
    grad_other, along_other = moved[:half], moved[half : half + 1 + half_rows]
    text_along = (along[0] + along_other[0])[:, None]
    keep_along = along[1:].reshape(-1)[:half, None]
    send_along = along_other[1:].reshape(-1)[:half, None]

    text_mine = lax.optimization_barrier(dot(grad, keep_unit, ((0,), (0,))))
    text_parts = []
    for k in range(2):
        cols = slice(k * (feat // 2), (k + 1) * (feat // 2))
        cot = text_mine[:, cols] + dot(grad_other, send_unit[:, cols], ((0,), (0,)))
        text_parts.append((scale * cot - text_unit[:, cols] * text_along) * text_inverse)
    text_back = [one + swap(one, near) for one in text_parts]
    keep_back = (scale * dot(grad, text_unit, ((1,), (0,))) - keep_unit * keep_along) * keep_inverse
    send_back = (scale * dot(grad_other, text_unit, ((1,), (0,))) - send_unit * send_along) * send_inverse
    clip_back = scatter_blocks(
        [
            jnp.concatenate([keep_back[q * part : (q + 1) * part], send_back[q * part : (q + 1) * part]], axis=0)
            for q in range(blocks)
        ],
        moves,
    )
    grad_clip = jnp.where(own_core == 0, clip_back, jnp.concatenate([clip_back[part:], clip_back[:part]], axis=0))

    top = blocks // 2
    outer = [q for q in range(blocks) if q & 1]
    inner = [q for q in range(blocks) if not q & 1]

    def hidden_of(which):
        return jnp.concatenate([hidden_tile[:, q * slot : (q + 1) * slot] for q in which], axis=1)

    halves = []
    for k in range(2):
        crossing = dot(hidden_of(outer), text_back[k], ((0,), (0,)))
        crossing = scatter_blocks([crossing[j * slot : (j + 1) * slot] for j in range(top)], moves[1:])
        halves.append(swap(crossing, moves[0]))
    text_back = jnp.concatenate(text_back, axis=1)
    rest = dot(hidden_of(inner), text_back, ((0,), (0,)))
    rest = scatter_blocks([rest[j * slot : (j + 1) * slot] for j in range(top)], moves[1:])
    grad_weight = rest + jnp.concatenate(halves, axis=1)

    own_back = lax.dynamic_slice_in_dim(text_back, upper * rows, rows)
    hidden_part = dot(own_back, proj_weight, ((1,), (1,)))
    piece = width // proj_n
    hidden_parts = [
        lax.dynamic_slice_in_dim(hidden_part, (own_proj ^ (2 * (q & 1) + (q >> 1))) * piece, piece, axis=1)
        for q in range(proj_n)
    ]
    grad_hidden = scatter_blocks(hidden_parts, [far, core])
    return (grad_hidden, grad_weight, grad_clip)


def solution(mesh):
    in_specs = (
        P(("txt", "clip"), None),
        P(None, "proj"),
        P(("txt", "clip"), "proj"),
        P(("txt", "clip")),
        P(),
    )
    out_specs = (P(("txt", "clip"), "proj"), P(("txt", "clip"), "proj"), P(("txt", "clip"), "proj"))
    return jax.shard_map(body, mesh=mesh, in_specs=in_specs, out_specs=out_specs, check_vma=False)
```
